32 devices in a mesh: pair: 2 (over x), seq: 4 (over z), head: 4 (over y, core).
Axes of the slice: x: 2, y: 2, z: 4, core: 2. Of those that a mesh axis runs over, the one named last changes fastest.
Arguments:
- resp_query: bfloat16 [2, 4, 256, 4096], P('pair', 'seq', None, 'head'), may hold values from -6 to 6
- resp_key: bfloat16 [2, 4, 256, 1024], P('pair', 'seq', None, 'head'), may hold values from -6 to 6
- resp_value: bfloat16 [2, 4, 256, 1024], P('pair', 'seq', None, 'head'), may hold values from -6 to 6
- direction: bfloat16 [2, 4, 256, 4096], P('pair', 'seq', None, 'head'), may hold values from -96 to 96
- ratio: float32 [2, 4, 256], P('pair', 'seq'), may hold values from -4.2 to 4.2
- lengths: int32 [2, 4], P('pair', 'seq'), may hold values from 1 to 256, 640 in all within a row
- partner: int32 [4], replicated, may hold values from 0 to 3, each once
- prompt_key: bfloat16 [1024, 1024], P('pair', 'head'), may hold values from -6 to 6
- prompt_value: bfloat16 [1024, 1024], P('pair', 'head'), may hold values from -6 to 6
Outputs:
- query_grad: bfloat16 [2, 4, 256, 4096], P('pair', 'seq', None, 'head')
- resp_key_grad: bfloat16 [2, 4, 256, 1024], P('pair', 'seq', None, 'head')
- resp_value_grad: bfloat16 [2, 4, 256, 1024], P('pair', 'seq', None, 'head')
- prompt_key_grad: bfloat16 [1024, 1024], P('pair', 'head')
- prompt_value_grad: bfloat16 [1024, 1024], P('pair', 'head')
The draws below stay inside these ranges and needn't reach their ends.
Inputs may be any that keep to these rules, and one draw needn't show every extreme that they name: On each side the response lengths sum to 640, and the longest is 256. partner names each rejected response exactly once.
All inputs are finite; a program needn't handle non-finite values. No bound on the sum of `lengths` on one device may be relied on, other than what follows from the above.
Results may differ from the reference program's by a relative error of at most 0.03.
Values may be sent and summed in bfloat16 or wider, within the bound.
A program may use at most 64 MiB of HBM per device.

```python
import math
import jax
import jax.numpy as jnp
import numpy as np
from jax import lax

KV_HEADS = 8
HEAD_DIM = 128
GROUP_WIN = 4
RESP = 256
HEADS = 32
RESPONSES = 4
PROMPT = 1024


def draw_resp_query(key, part):
    full_shape = (2, RESPONSES, RESP, KV_HEADS * GROUP_WIN * HEAD_DIM)
    drawn = jnp.clip(jax.random.normal(key, full_shape, jnp.float32), -6.0, 6.0)
    return drawn.astype(jnp.bfloat16)


def draw_prompt_key(key, part):
    full_shape = (PROMPT, KV_HEADS * HEAD_DIM)
    drawn = jnp.clip(jax.random.normal(key, full_shape, jnp.float32), -6.0, 6.0)
    return drawn.astype(jnp.bfloat16)


def draw_ratio(key, part):
    full_shape = (2, RESPONSES, RESP)
    resp_rank = jnp.arange(RESPONSES, dtype=jnp.float32)
    spread = 0.4 * (1.0 + 2.0 * resp_rank / max(RESPONSES - 1, 1))
    drawn = jnp.clip(jax.random.normal(key, full_shape, jnp.float32), -3.5, 3.5)
    return (drawn * spread[None, :, None]).astype(jnp.float32)


def block_levels(stream_key, extent, pieces, smallest, largest):
    factor_of = 1.0
    for dim, blocks in pieces:
        draws = jax.random.uniform(jax.random.fold_in(jax.random.fold_in(stream_key, 6), dim), (blocks,), jnp.float32, smallest / len(pieces), largest / len(pieces))
        factor_of = factor_of * jnp.repeat(jnp.exp(draws), extent[dim] // blocks).reshape((-1,) + (1,) * (len(extent) - 1 - dim))
    return factor_of


def length_profile(number_of, total, reach, lean):
    portions = [(1 << 20) // math.isqrt(grade ** lean) + 1 for grade in range(2, number_of + 1)]
    spare, holding = total - reach - (number_of - 1), [1] * (number_of - 1)
    while spare > 0:
        free = [i for i in range(number_of - 1) if holding[i] < reach]
        pool, left = sum([portions[i] for i in free]), spare
        for i in free:
            more = min(reach - holding[i], max(1, left * portions[i] // pool), spare)
            holding[i] = holding[i] + more
            spare = spare - more
    return np.array([reach] + holding)


def uneven(rng, amount, total, reach, slope):
    if amount == 2:
        one = jax.random.randint(rng, (), max(1, total - reach), min(reach, total - 1) + 1)
        return jnp.stack([one, total - one])
    sizes = jnp.asarray(length_profile(amount, total, reach, slope), jnp.int32)
    couples = (amount - 1) // 2
    donor, sink = sizes[1:1 + 2 * couples:2], sizes[2:2 + 2 * couples:2]
    margin = jnp.minimum(donor - 1, reach - sink)
    passed = jax.random.randint(jax.random.fold_in(rng, 1), (couples,), 0, 1 << 20) % (margin + 1)
    sizes = sizes.at[1:1 + 2 * couples:2].set(donor - passed).at[2:2 + 2 * couples:2].set(sink + passed)
    return sizes[jax.random.permutation(jax.random.fold_in(rng, 2), amount)]


def gaussian(rng, dims, scale, most, cuts=(), held_as=jnp.bfloat16):
    result = scale * jax.random.normal(rng, dims, jnp.float32)
    if cuts:
        result = result * block_levels(rng, dims, cuts, -0.22, 0.18)
    return jnp.clip(result, -most, most).astype(held_as)


def setup_inputs(seed: int = 0) -> dict:
    keys = jax.random.split(jax.random.key(seed), 10)
    resp_query = draw_resp_query(jax.random.fold_in(keys[9], 71), 0)
    resp_key = gaussian(keys[1], (2, RESPONSES, RESP, KV_HEADS * HEAD_DIM), 1.0, 6.0, ((0, 2), (1, 4), (3, 4)))
    resp_value = gaussian(keys[2], (2, RESPONSES, RESP, KV_HEADS * HEAD_DIM), 1.0, 6.0, ((0, 2), (1, 4), (3, 4)))
    direction = gaussian(keys[3], (2, RESPONSES, RESP, HEADS * HEAD_DIM), 16.0, 96.0, ((0, 2), (1, 4), (3, 4)))
    ratio = draw_ratio(jax.random.fold_in(keys[9], 71), 0)
    lengths = jax.vmap(lambda own: uneven(own, RESPONSES, 5 * RESPONSES * RESP // 8, RESP, 2))(jax.random.split(keys[5], 2)).reshape((2, RESPONSES)).astype(jnp.int32)
    partner = jax.random.permutation(keys[6], RESPONSES).astype(jnp.int32)
    prompt_key = draw_prompt_key(jax.random.fold_in(keys[9], 71), 0)
    prompt_value = gaussian(keys[8], (PROMPT, KV_HEADS * HEAD_DIM), 1.0, 6.0, ((0, 2), (1, 4)))
    return dict(resp_query=resp_query, resp_key=resp_key, resp_value=resp_value, direction=direction, ratio=ratio, lengths=lengths, partner=partner, prompt_key=prompt_key, prompt_value=prompt_value)


dpo_beta = 0.1

def attend(query_rows, resp_k, resp_v, cot_rows, length, prompt_k, prompt_v):
    resp_rows = query_rows.shape[0]
    prompt_rows = prompt_k.shape[0]
    score_scale = 1.0 / math.sqrt(HEAD_DIM)
    positions = jnp.arange(resp_rows, dtype=jnp.int32)
    causal = (positions[None, :] <= positions[:, None]) & (positions[None, :] < length)
    visible = jnp.concatenate([jnp.ones((resp_rows, prompt_rows), dtype=jnp.bool_), causal], axis=1)
    query_parts, key_parts, value_parts, prompt_key_parts, prompt_value_parts = ([], [], [], [], [])
    for kv_index in range(KV_HEADS):
        head_cols = slice(kv_index * GROUP_WIN * HEAD_DIM, (kv_index + 1) * GROUP_WIN * HEAD_DIM)
        key_cols = slice(kv_index * HEAD_DIM, (kv_index + 1) * HEAD_DIM)
        key_rows = jnp.concatenate([prompt_k[:, key_cols], resp_k[:, key_cols]], 0).astype(jnp.float32)
        value_rows = jnp.concatenate([prompt_v[:, key_cols], resp_v[:, key_cols]], 0).astype(jnp.float32)
        query_f = query_rows[:, head_cols].reshape(resp_rows, GROUP_WIN, HEAD_DIM).astype(jnp.float32)
        grad_f = cot_rows[:, head_cols].reshape(resp_rows, GROUP_WIN, HEAD_DIM).astype(jnp.float32)
        scores = jnp.einsum('sgd,kd->sgk', query_f, key_rows) * score_scale
        scores = jnp.where(visible[:, None, :], scores, -jnp.inf)
        row_max = lax.optimization_barrier(jnp.max(scores, axis=2, keepdims=True))
        exponent = jnp.exp(scores - row_max)
        attn_prob = exponent / lax.optimization_barrier(jnp.sum(exponent, axis=2, keepdims=True))
        prob_half = lax.optimization_barrier(attn_prob.astype(jnp.bfloat16)).astype(jnp.float32)
        attended = jnp.einsum('sgk,kd->sgd', prob_half, value_rows)
        attended = lax.optimization_barrier(attended.astype(jnp.bfloat16)).astype(jnp.float32)
        row_delta = lax.optimization_barrier(jnp.sum(grad_f * attended, axis=2, keepdims=True))
        prob_grad = jnp.einsum('sgd,kd->sgk', grad_f, value_rows)
        score_grad = lax.optimization_barrier((attn_prob * (prob_grad - row_delta)).astype(jnp.bfloat16)).astype(jnp.float32)
        query_out = (jnp.einsum('sgk,kd->sgd', score_grad, key_rows) * score_scale).astype(jnp.bfloat16)
        query_parts.append(query_out.reshape(resp_rows, GROUP_WIN * HEAD_DIM))
        key_term = jnp.einsum('sgk,sgd->kd', score_grad, query_f) * score_scale
        value_term = jnp.einsum('sgk,sgd->kd', prob_half, grad_f)
        prompt_key_parts.append(key_term[:prompt_rows])
        prompt_value_parts.append(value_term[:prompt_rows])
        key_parts.append(key_term[prompt_rows:].astype(jnp.bfloat16))
        value_parts.append(value_term[prompt_rows:].astype(jnp.bfloat16))
    return (jnp.concatenate(query_parts, 1), jnp.concatenate(key_parts, 1), jnp.concatenate(value_parts, 1), jnp.concatenate(prompt_key_parts, 1), jnp.concatenate(prompt_value_parts, 1))

def flatten(array):
    return array.reshape((-1,) + array.shape[2:])

def reference(resp_query, resp_key, resp_value, direction, ratio, lengths, partner, prompt_key, prompt_value):
    positions = jnp.arange(ratio.shape[2], dtype=jnp.int32)
    live_mask = positions[None, None, :] < lengths[:, :, None]
    seq_sums = lax.optimization_barrier(jnp.sum(jnp.where(live_mask, ratio, 0.0), axis=2))
    pulled = jax.nn.sigmoid(-(dpo_beta * (seq_sums[0] - seq_sums[1][partner])))
    rejected = jnp.zeros_like(pulled).at[partner].set(pulled)
    weight = jnp.stack([-pulled, rejected])
    out_grads = jnp.where(live_mask[..., None], weight[:, :, None, None] * direction.astype(jnp.float32), 0.0).astype(jnp.bfloat16)

    def per_response(totals, inputs):
        query_rows, resp_k, resp_v, cot_rows, length = inputs
        query_out, key_out, value_out, prompt_kt, prompt_vt = attend(query_rows, resp_k, resp_v, cot_rows, length, prompt_key, prompt_value)
        return ((totals[0] + prompt_kt, totals[1] + prompt_vt), (query_out, key_out, value_out))
    zeros_init = jnp.zeros(prompt_key.shape, jnp.float32)
    (prompt_kt, prompt_vt), (query_out, key_out, value_out) = lax.scan(per_response, (zeros_init, zeros_init), (flatten(resp_query), flatten(resp_key), flatten(resp_value), flatten(out_grads), lengths.reshape(-1)))
    return (query_out.reshape(resp_query.shape), key_out.reshape(resp_key.shape), value_out.reshape(resp_value.shape), prompt_kt.astype(jnp.bfloat16), prompt_vt.astype(jnp.bfloat16))
```

```python
import functools
import math

import jax
import jax.numpy as jnp
from jax import lax
from jax.experimental import pallas as pl
from jax.experimental.pallas import tpu as pltpu
from jax.sharding import PartitionSpec as P

HEAD_DIM = 128
DPO_BETA = 0.1
UNIT = 128
SLAB = 8
LAGS = (4, 8, 12)
PER_SLOT = 2
MESH = pl.DeviceIdType.MESH
NT = (((1,), (1,)), ((), ()))
TN = (((0,), (0,)), ((), ()))
F32 = jnp.float32
BF16 = jnp.bfloat16


def dot_nt(a, b):
    return lax.dot_general(a, b, NT, preferred_element_type=F32)


def dot_tn(a, b):
    return lax.dot_general(a, b, TN, preferred_element_type=F32)


def sizes(n, half):
    paired = n % 2 == 0
    part = half // 2
    return paired, part, part // 2, min(UNIT, part)


def kernel(
    n, lengths_in, partner_in, ratio_in, q_in, rk_in, rv_in, dir_in, pk_in, pv_in,
    qg_out, rkg_out, rvg_out, pkg_out, pvg_out,
    lengths, partner, ratio, table, held, pk_far, pv_far,
    s_buf, dp_buf, ds_buf, x_send, x_recv, acc, c_send, c_recv,
    small_sem, load_sem, tab_send_sem, tab_recv_sem, pair_sem,
    near_send_sem, near_recv_sem, relay_send_sem, relay_recv_sem,
    x_send_sem, x_recv_sem, c_send_sem, c_recv_sem,
):
    ns = jax.named_scope
    rows = q_in.shape[2]
    half = pk_in.shape[0]
    kv_local = rk_in.shape[3] // HEAD_DIM
    group = q_in.shape[3] // rk_in.shape[3]
    lanes = rows * group
    paired, part, chunk, unit = sizes(n, half)
    units = half // unit
    per_part = part // unit
    count = 2 * kv_local * units
    scale = 1.0 / math.sqrt(HEAD_DIM)
    exp_scale = scale * math.log2(math.e)
    side = lax.axis_index("pair")
    seq = lax.axis_index("seq")
    head = lax.axis_index("head")
    flat = side * n + seq
    parity = lax.rem(seq, 2)
    pair_dev = (1 - side, seq, head)

    def seq_dev(way):
        return (side, lax.rem(seq + way + n, n), head)

    def exists(way):
        return (seq + way >= 0) & (seq + way < n)

    barrier = pltpu.get_barrier_semaphore()
    pl.semaphore_signal(barrier, inc=1, device_id=pair_dev, device_id_type=MESH)
    for way in (1, -1):
        @pl.when(exists(way))
        def _():
            pl.semaphore_signal(barrier, inc=1, device_id=seq_dev(way), device_id_type=MESH)

    def cols_of(k):
        return slice(k * HEAD_DIM, (k + 1) * HEAD_DIM)

    small = [
        pltpu.make_async_copy(ratio_in, ratio, small_sem.at[0]),
        pltpu.make_async_copy(lengths_in, lengths, small_sem.at[1]),
        pltpu.make_async_copy(partner_in, partner, small_sem.at[2]),
    ]
    at_q = half
    at_rk = at_q + lanes
    at_g = at_rk + rows
    at_pv = at_g + lanes
    at_rv = at_pv + half
    groups = ((0, at_q), (at_q, at_g), (at_g, at_rv + rows))
    small[0].start()
    small[1].start()
    for i in range(kv_local):
        loads = [(pk_in.at[:, cols_of(i)], 0, half, 0)]
        for g in range(group):
            loads.append((q_in.at[0, 0, :, cols_of(i * group + g)], at_q + g * rows, rows, 1))
        loads.append((rk_in.at[0, 0, :, cols_of(i)], at_rk, rows, 1))
        loads.append((pv_in.at[:, cols_of(i)], at_pv, half, 2))
        for g in range(group):
            loads.append((dir_in.at[0, 0, :, cols_of(i * group + g)], at_g + g * rows, rows, 2))
        loads.append((rv_in.at[0, 0, :, cols_of(i)], at_rv, rows, 2))
        for src, at, size, which in loads:
            pltpu.make_async_copy(src, held.at[i, at:at + size, :], load_sem.at[3 * i + which]).start()
    small[2].start()

    def loaded(i, which):
        with ns("loads"):
            whole = held.at[i, groups[which][0]:groups[which][1], :]
            pltpu.make_async_copy(whole, whole, load_sem.at[3 * i + which]).wait()

    def queries(i):
        return held[i, at_q:at_q + lanes, :]

    def grads(i):
        return held[i, at_g:at_g + lanes, :]

    def near_rows(i, at, name):
        at, size = (at[1], rows) if name == "resp" else (at[0] + name * part, part)
        return held[i, at:at + size, :]

    direct, relayed = {}, {}
    for i in range(kv_local):
        for which, (at, dst) in enumerate(((0, pk_far), (at_pv, pv_far))):
            slot = 2 * i + which
            if paired and slot > 0:
                size, first = chunk, parity * part
            else:
                size, first = half, 0
            direct[slot], relayed[slot] = [], []
            for c in range(2 if size == chunk else 1):
                row = pl.multiple_of(first + c * size, size)
                span = pl.ds(row, size)
                direct[slot].append(pltpu.make_async_remote_copy(
                    src_ref=held.at[i, pl.ds(pl.multiple_of(at + row, chunk), size), :], dst_ref=dst.at[i, span, :],
                    send_sem=near_send_sem.at[slot], recv_sem=near_recv_sem.at[2 * slot + c],
                    device_id=pair_dev, device_id_type=MESH))
                if size == chunk:
                    relayed[slot].append(pltpu.make_async_remote_copy(
                        src_ref=dst.at[i, span, :], dst_ref=dst.at[i, span, :],
                        send_sem=relay_send_sem.at[slot], recv_sem=relay_recv_sem.at[slot],
                        device_id=(side, lax.rem(seq + 1 - 2 * parity + n, n), head),
                        device_id_type=MESH))

    def whole_of(slot, send_sem, recv_sem, first):
        i, which = slot // 2, slot % 2
        span = pl.ds(pl.multiple_of(first * part, part), part)
        ref = (pk_far, pv_far)[which].at[i, span, :]
        return pltpu.make_async_remote_copy(
            src_ref=ref, dst_ref=ref, send_sem=send_sem.at[slot], recv_sem=recv_sem.at[slot],
            device_id=pair_dev, device_id_type=MESH)

    def give(slot):
        for copy in direct[slot]:
            copy.start()

    def relay(slot, c):
        with ns("relay"):
            direct[slot][c].wait_recv()
            if relayed[slot]:
                relayed[slot][c].start()

    def relay_all(slot):
        for c in range(len(direct[slot])):
            relay(slot, c)

    def wait_far(slot):
        if relayed[slot]:
            with ns("wait2"):
                whole_of(slot, relay_send_sem, relay_recv_sem, 1 - parity).wait_recv()

    def sent_far(slot):
        if relayed[slot]:
            whole_of(slot, near_send_sem, relay_recv_sem, parity).wait_send()
            whole_of(slot, relay_send_sem, relay_recv_sem, parity).wait_send()
        else:
            direct[slot][0].wait_send()

    tab_pair = pltpu.make_async_remote_copy(
        src_ref=table.at[seq, side], dst_ref=table.at[seq, side],
        send_sem=pair_sem.at[0], recv_sem=pair_sem.at[1],
        device_id=pair_dev, device_id_type=MESH)

    def tab_copy(k, way):
        turn = (1 - way) // 2
        return pltpu.make_async_remote_copy(
            src_ref=table.at[seq - way * k], dst_ref=table.at[seq - way * k],
            send_sem=tab_send_sem.at[turn], recv_sem=tab_recv_sem.at[2 * k + turn],
            device_id=seq_dev(way), device_id_type=MESH)

    def came_from(k, way):
        return (seq - way * k >= 0) & (seq - way * k < n)

    def tab_step(k):
        if k == 0:
            tab_pair.wait_recv()
        for way in (1, -1):
            if k > 0:
                @pl.when(came_from(k, way))
                def _():
                    tab_copy(k - 1, way).wait_recv()

                @pl.when(came_from(k - 1, way) & exists(way))
                def _():
                    tab_copy(k - 1, way).wait_send()
            if k < n - 1:
                @pl.when(came_from(k, way) & exists(way))
                def _():
                    tab_copy(k, way).start()

    steps = list(range(n))
    per_call = -(-(n - 1) // 3)

    def tab_some(all_left=False):
        with ns("tab"):
            for _ in range(n if all_left else per_call if steps and steps[0] else 1):
                if steps:
                    tab_step(steps.pop(0))

    def weights():
        zero = jnp.zeros((1, HEAD_DIM), F32)
        mine = partner[seq]
        rejected, chosen = zero, zero
        for r in range(n):
            rejected = rejected + jnp.where(mine == r, table[r, 1], 0.0)
            chosen = chosen + jnp.where(partner[r] == seq, table[r, 0], 0.0)
        pulled_c = 1.0 / (1.0 + jnp.exp(DPO_BETA * (table[seq, 0] - rejected)))
        pulled_r = 1.0 / (1.0 + jnp.exp(DPO_BETA * (chosen - table[seq, 1])))
        own = jnp.where(side == 0, -pulled_c, pulled_r)
        other = jnp.where(side == 0, pulled_r, -pulled_c)
        return own, other

    far_at, own_at, resp_at = 0, half, 2 * half

    def score(i, at, keys, masked=False):
        scores = dot_nt(keys, queries(i))
        if masked:
            key_pos = lax.broadcasted_iota(jnp.int32, scores.shape, 0)
            row_pos = lax.rem(lax.broadcasted_iota(jnp.int32, scores.shape, 1), rows)
            scores = jnp.where((key_pos <= row_pos) & (key_pos < length), scores, -jnp.inf)
        size = scores.shape[0]
        s_buf[i, at:at + size, :] = scores
        top = jnp.max(scores, axis=0, keepdims=True)
        shift = top * exp_scale
        total = jnp.zeros((SLAB, lanes), F32)
        for r in range(0, size, SLAB):
            span = slice(at + r, at + r + SLAB)
            e = jnp.exp2(s_buf[i, span, :] * exp_scale - shift)
            s_buf[i, span, :] = e
            total = total + e
        return top, jnp.sum(total, axis=0, keepdims=True)

    def prob_grad(i, at, values):
        dp = dot_nt(values, grads(i))
        size = dp.shape[0]
        dp_buf[i, at:at + size, :] = dp
        total = jnp.zeros((SLAB, lanes), F32)
        for r in range(0, size, SLAB):
            span = slice(at + r, at + r + SLAB)
            total = total + s_buf[i, span, :] * dp[r:r + SLAB]
        return jnp.sum(total, axis=0, keepdims=True)

    def value_grad(i, at, size, share):
        prob = (s_buf[i, at:at + size, :] * share).astype(BF16)
        return jnp.dot(prob, grads(i), preferred_element_type=F32)

    def key_grad(i, at, size, share, delta):
        ds = (s_buf[i, at:at + size, :] * share * (dp_buf[i, at:at + size, :] - delta)).astype(BF16)
        ds_buf[i, at:at + size, :] = ds
        return jnp.dot(ds, queries(i), preferred_element_type=F32)

    def unit_of(i, kind, r):
        return (2 * i + kind) * units + r

    def x_copy(u):
        return pltpu.make_async_remote_copy(
            src_ref=x_send.at[u], dst_ref=x_recv.at[u],
            send_sem=x_send_sem.at[0], recv_sem=x_recv_sem.at[u],
            device_id=pair_dev, device_id_type=MESH)

    def send_far(i, kind, b, grads):
        for k in range(per_part):
            u = unit_of(i, kind, b * per_part + k)
            x_send[u] = grads[k * unit:(k + 1) * unit].astype(BF16)
            x_copy(u).start()

    def keep_own(i, kind, b, grads):
        for k in range(per_part):
            acc[unit_of(i, kind, b * per_part + k)] = grads[k * unit:(k + 1) * unit]

    first_way = jnp.where(2 * seq < n, 1, -1)

    def chain_copy(u, way):
        turn = (1 - way) // 2
        return pltpu.make_async_remote_copy(
            src_ref=c_send.at[turn, u], dst_ref=c_recv.at[turn, u],
            send_sem=c_send_sem.at[turn], recv_sem=c_recv_sem.at[2 * u + turn],
            device_id=seq_dev(way), device_id_type=MESH)

    def chain_pass(u, way):
        turn = (1 - way) // 2
        chain_copy(u, way).wait_recv()
        c_send[turn, u] = (acc[u] + c_recv[turn, u].astype(F32)).astype(BF16)
        chain_copy(u, way).start()

    def chain_enter(u, own, other):
        factor = scale if (u // units) % 2 else 1.0
        with ns("xwait"):
            x_copy(u).wait_recv()
        acc[u] = acc[u] * (own * factor) + x_recv[u].astype(F32) * (other * factor)

        @pl.when(exists(first_way) & jnp.logical_not(exists(-first_way)))
        def _():
            c_send[(1 - first_way) // 2, u] = acc[u].astype(BF16)
            chain_copy(u, first_way).start()

    def chain_inward(u):
        @pl.when(exists(first_way) & exists(-first_way))
        def _():
            with ns("inward"):
                chain_pass(u, first_way)

    def chain_outward(u):
        @pl.when(exists(first_way) & exists(-first_way))
        def _():
            with ns("outward"):
                chain_pass(u, -first_way)
            write(u)

    def chain_end(u):
        @pl.when(jnp.logical_not(exists(-first_way)))
        def _():
            @pl.when(exists(first_way))
            def _():
                with ns("endwait"):
                    chain_copy(u, -first_way).wait_recv()
            write(u)

    def write(u):
        for way in (1, -1):
            @pl.when(exists(-way))
            def _():
                acc[u] += c_recv[(1 - way) // 2, u].astype(F32)
        i, kind, r = u // (2 * units), u // units % 2, u % units
        out = pkg_out if kind else pvg_out
        out[r * unit:(r + 1) * unit, cols_of(i)] = acc[u].astype(BF16)

    def slot(s, own, other):
        for lag, step in zip(LAGS[::-1], (chain_end, chain_outward, chain_inward)):
            if 0 <= s - lag < count:
                step(s - lag)
        if s < count:
            chain_enter(s, own, other)

    def query(i, own):
        total = jnp.zeros((HEAD_DIM, lanes), F32)
        for at, keys in (
            (own_at, held[i, :half, :]), (resp_at, held[i, at_rk:at_rk + rows, :]), (far_at, pk_far[i])
        ):
            total = total + dot_tn(keys, ds_buf[i, at:at + keys.shape[0], :])
        factor = own * scale
        for g in range(group):
            qg_out[0, 0, :, cols_of(i * group + g)] = (
                total[:, g * rows:(g + 1) * rows].T * factor).astype(BF16)

    def resp(i, own):
        rvg_out[0, 0, :, cols_of(i)] = (
            value_grad(i, resp_at, rows, share[i, "resp"]) * own).astype(BF16)
        rkg_out[0, 0, :, cols_of(i)] = (
            key_grad(i, resp_at, rows, share[i, "resp"], delta[i]) * (own * scale)).astype(BF16)

    tops, totals, deltas, share, delta = {}, {}, {}, {}, {}

    def at_of(name):
        return resp_at if name == "resp" else own_at + name * part

    def near(i, name):
        with ns(f"near{i}{name}"):
            tops[i, name], totals[i, name] = score(
                i, at_of(name), near_rows(i, (0, at_rk), name), name == "resp")

    def near_delta(i, name):
        with ns(f"dnear{i}{name}"):
            deltas[i, name] = prob_grad(i, at_of(name), near_rows(i, (at_pv, at_rv), name))

    def far(i, b):
        with ns(f"far{i}{b}"):
            at = far_at + b * part
            tops[i, f"far{b}"], totals[i, f"far{b}"] = score(i, at, pk_far[i, b * part:(b + 1) * part, :])

    def far_delta(i, b):
        with ns(f"dfar{i}{b}"):
            at = far_at + b * part
            deltas[i, f"far{b}"] = prob_grad(i, at, pv_far[i, b * part:(b + 1) * part, :])

    names = ("far0", "far1", 0, 1, "resp")

    def stats(i):
        top = functools.reduce(jnp.maximum, [tops[i, name] for name in names])
        part_of = {name: jnp.exp2((tops[i, name] - top) * exp_scale) for name in names}
        total = sum(totals[i, name] * part_of[name] for name in names)
        row = lax.rem(lax.broadcasted_iota(jnp.int32, (1, lanes), 1), rows)
        inv = jnp.where(row < length, 1.0 / total, 0.0)
        for name in names:
            share[i, name] = part_of[name] * inv

    def far_values(i, b):
        with ns(f"vfar{i}{b}"):
            send_far(i, 0, b, value_grad(i, far_at + b * part, part, share[i, f"far{b}"]))

    def far_keys(i, b):
        with ns(f"kfar{i}{b}"):
            send_far(i, 1, b, key_grad(i, far_at + b * part, part, share[i, f"far{b}"], delta[i]))

    def own_values(i, b):
        with ns(f"vown{i}{b}"):
            keep_own(i, 0, b, value_grad(i, own_at + b * part, part, share[i, b]))

    def own_keys(i, b):
        with ns(f"kown{i}{b}"):
            keep_own(i, 1, b, key_grad(i, own_at + b * part, part, share[i, b], delta[i]))

    def sum_delta(i):
        delta[i] = sum(deltas[i, name] * share[i, name] for name in names)

    with ns("small"):
        small[0].wait()
        small[1].wait()
    length = lengths[0, 0]
    position = lax.broadcasted_iota(jnp.int32, (1, rows), 1)
    own_sum = jnp.sum(jnp.where(position < length, ratio[0], 0.0), axis=1, keepdims=True)
    table[seq, side] = jnp.broadcast_to(own_sum, (1, HEAD_DIM))
    with ns("barrier"):
        pl.semaphore_wait(barrier, 1 + jnp.where(exists(1), 1, 0) + jnp.where(exists(-1), 1, 0))
    tab_pair.start()
    loaded(0, 0)
    give(0)
    last = kv_local - 1
    loaded(0, 1)
    near(0, 0)
    loaded(0, 2)
    give(1)
    for i in range(1, kv_local):
        for which in range(3):
            loaded(i, which)
        give(2 * i)
        give(2 * i + 1)
    near(0, 1)
    near(0, "resp")
    tab_some()
    if last:
        near(last, 0)
        near(last, 1)
        near(last, "resp")
    near_delta(0, 0)
    near_delta(0, 1)
    tab_some()
    near_delta(0, "resp")
    relay_all(0)
    far(0, 0)
    relay(1, 0)
    far(0, 1)
    stats(0)
    if len(direct[1]) > 1:
        relay(1, 1)
    far_values(0, 0)
    far_values(0, 1)
    tab_some()
    if last:
        relay_all(2 * last)
    own_values(0, 0)
    own_values(0, 1)
    wait_far(1)
    far_delta(0, 0)
    far_delta(0, 1)
    sum_delta(0)
    far_keys(0, 0)
    far_keys(0, 1)
    tab_some(True)
    with ns("small"):
        small[2].wait()
    own, other = weights()

    def resp_work(i):
        with ns(f"resp{i}"):
            resp(i, own)

    def query_work(i):
        with ns(f"query{i}"):
            query(i, own)

    work = [lambda: own_keys(0, 0), lambda: own_keys(0, 1)]
    if last:
        work += [
            lambda: relay_all(2 * last + 1),
            lambda: near_delta(last, 0), lambda: near_delta(last, 1), lambda: near_delta(last, "resp"),
            lambda: (wait_far(2 * last), far(last, 0)), lambda: (far(last, 1), stats(last)),
            lambda: far_values(last, 0), lambda: far_values(last, 1),
            lambda: (wait_far(2 * last + 1), far_delta(last, 0)),
            lambda: (far_delta(last, 1), sum_delta(last)),
            lambda: far_keys(last, 0), lambda: far_keys(last, 1),
            lambda: own_values(last, 0), lambda: own_values(last, 1),
            lambda: own_keys(last, 0), lambda: own_keys(last, 1),
        ]
    work += [lambda i=i: resp_work(i) for i in range(kv_local)]
    work += [lambda i=i: query_work(i) for i in range(kv_local)]
    for s in range(count + LAGS[-1]):
        slot(s, own, other)
        for _ in range(PER_SLOT):
            if work:
                work.pop(0)()
    while work:
        work.pop(0)()

    with ns("sendwait"):
        tab_pair.wait_send()
        for slot_ in range(2 * kv_local):
            sent_far(slot_)
        pltpu.make_async_remote_copy(
            src_ref=x_send, dst_ref=x_recv, send_sem=x_send_sem.at[0], recv_sem=x_recv_sem.at[0],
            device_id=pair_dev, device_id_type=MESH).wait_send()
        for way in (1, -1):
            @pl.when(exists(way))
            def _():
                turn = (1 - way) // 2
                pltpu.make_async_remote_copy(
                    src_ref=c_send.at[turn], dst_ref=c_recv.at[turn],
                    send_sem=c_send_sem.at[turn], recv_sem=c_recv_sem.at[0],
                    device_id=seq_dev(way), device_id_type=MESH).wait_send()


def store_kernel(count, *refs):
    sources, targets, sem = refs[:count], refs[count:2 * count], refs[2 * count]
    stores = [pltpu.make_async_copy(sources[k], targets[k], sem.at[k]) for k in range(count)]
    for store in stores:
        store.start()
    for store in stores:
        store.wait()


def store_all(arrays):
    count = len(arrays)
    return pl.pallas_call(
        functools.partial(store_kernel, count),
        out_shape=tuple(jax.ShapeDtypeStruct(a.shape, a.dtype) for a in arrays),
        in_specs=[pl.BlockSpec(memory_space=pltpu.VMEM)] * count,
        out_specs=(pl.BlockSpec(memory_space=pl.ANY),) * count,
        scratch_shapes=[pltpu.SemaphoreType.DMA((count,))],
        compiler_params=pltpu.CompilerParams(vmem_limit_bytes=1024 * 1024),
        name="store_results",
    )(*arrays)


def shards(
    n, resp_query, resp_key, resp_value, direction, ratio, lengths, partner, prompt_key, prompt_value
):
    rows = resp_query.shape[2]
    half, key_width = prompt_key.shape
    kv_local = key_width // HEAD_DIM
    heads = resp_query.shape[3] // HEAD_DIM
    lanes = rows * heads // kv_local
    keys = 2 * half + rows
    unit = sizes(n, half)[-1]
    count = 2 * kv_local * (half // unit)
    hbm = pl.BlockSpec(memory_space=pltpu.HBM)
    dma = pltpu.SemaphoreType.DMA
    results = pl.pallas_call(
        functools.partial(kernel, n),
        out_shape=tuple(
            pltpu.VMEM(a.shape, BF16)
            for a in (resp_query, resp_key, resp_value, prompt_key, prompt_value)
        ),
        in_specs=[hbm] * 9,
        scratch_shapes=[
            pltpu.SMEM((1, 1), jnp.int32),
            pltpu.SMEM((n,), jnp.int32),
            pltpu.VMEM((1, 1, rows), F32),
            pltpu.VMEM((n, 2, 1, HEAD_DIM), F32),
            pltpu.VMEM((kv_local, 2 * (half + lanes + rows), HEAD_DIM), BF16),
            pltpu.VMEM((kv_local, half, HEAD_DIM), BF16),
            pltpu.VMEM((kv_local, half, HEAD_DIM), BF16),
            pltpu.VMEM((kv_local, keys, lanes), F32),
            pltpu.VMEM((kv_local, keys, lanes), F32),
            pltpu.VMEM((kv_local, keys, lanes), BF16),
            pltpu.VMEM((count, unit, HEAD_DIM), BF16),
            pltpu.VMEM((count, unit, HEAD_DIM), BF16),
            pltpu.VMEM((count, unit, HEAD_DIM), F32),
            pltpu.VMEM((2, count, unit, HEAD_DIM), BF16),
            pltpu.VMEM((2, count, unit, HEAD_DIM), BF16),
            dma((3,)), dma((3 * kv_local,)), dma((2,)), dma((2 * max(n - 1, 1),)), dma((2,)),
            dma((2 * kv_local,)), dma((4 * kv_local,)), dma((2 * kv_local,)), dma((2 * kv_local,)),
            dma((1,)), dma((count,)), dma((2,)), dma((2 * count,)),
        ],
        compiler_params=pltpu.CompilerParams(
            collective_id=0, has_side_effects=True, vmem_limit_bytes=48 * 1024 * 1024
        ),
        name="shared_prompt_backward",
    )(lengths, *(
        pltpu.with_memory_space_constraint(a, pltpu.HBM)
        for a in (partner, ratio, resp_query, resp_key, resp_value, direction, prompt_key, prompt_value)
    ))
    return store_all(results)


def solution(mesh):
    per_response = P("pair", "seq", None, "head")
    per_prompt = P("pair", "head")
    in_specs = (
        per_response, per_response, per_response, per_response,
        P("pair", "seq", None), P("pair", "seq"), P(), per_prompt, per_prompt,
    )
    out_specs = (per_response, per_response, per_response, per_prompt, per_prompt)
    return jax.shard_map(
        functools.partial(shards, mesh.shape["seq"]),
        mesh=mesh, in_specs=in_specs, out_specs=out_specs, check_vma=False,
    )
```

```python
import functools
import math

import jax
import jax.numpy as jnp
from jax import lax
from jax.experimental import pallas as pl
from jax.experimental.pallas import tpu as pltpu
from jax.sharding import PartitionSpec as P

HEAD_DIM = 128
DPO_BETA = 0.1
UNIT = 128
SLAB = 8
RATE, HOP, LEAD = 0.7, 3.5, 0.6
MESH = pl.DeviceIdType.MESH
NT = (((1,), (1,)), ((), ()))
TN = (((0,), (0,)), ((), ()))
F32 = jnp.float32
BF16 = jnp.bfloat16


def dot_nt(a, b):
    return lax.dot_general(a, b, NT, preferred_element_type=F32)


def dot_tn(a, b):
    return lax.dot_general(a, b, TN, preferred_element_type=F32)


def sizes(n, half):
    paired = n % 2 == 0
    part = half // 2
    return paired, part, part // 2, min(UNIT, part)


def kernel(
    n, lengths_in, partner_in, ratio_in, q_in, rk_in, rv_in, dir_in, pk_in, pv_in,
    qg_out, rkg_out, rvg_out, pkg_out, pvg_out,
    lengths, partner, ratio, table, held, pk_far, pv_far,
    s_buf, dp_buf, ds_buf, x_send, x_recv, acc, c_send, c_recv,
    small_sem, load_sem, tab_send_sem, tab_recv_sem, pair_sem,
    near_send_sem, near_recv_sem, relay_send_sem, relay_recv_sem,
    x_send_sem, x_recv_sem, c_send_sem, c_recv_sem,
):
    ns = jax.named_scope
    rows = q_in.shape[2]
    half = pk_in.shape[0]
    kv_local = rk_in.shape[3] // HEAD_DIM
    group = q_in.shape[3] // rk_in.shape[3]
    lanes = rows * group
    paired, part, chunk, unit = sizes(n, half)
    units = half // unit
    per_part = part // unit
    count = 2 * kv_local * units
    scale = 1.0 / math.sqrt(HEAD_DIM)
    exp_scale = scale * math.log2(math.e)
    side = lax.axis_index("pair")
    seq = lax.axis_index("seq")
    head = lax.axis_index("head")
    flat = side * n + seq
    parity = lax.rem(seq, 2)
    pair_dev = (1 - side, seq, head)

    def seq_dev(way):
        return (side, lax.rem(seq + way + n, n), head)

    def exists(way):
        return (seq + way >= 0) & (seq + way < n)

    barrier = pltpu.get_barrier_semaphore()
    pl.semaphore_signal(barrier, inc=1, device_id=pair_dev, device_id_type=MESH)
    for way in (1, -1):
        @pl.when(exists(way))
        def _():
            pl.semaphore_signal(barrier, inc=1, device_id=seq_dev(way), device_id_type=MESH)

    def cols_of(k):
        return slice(k * HEAD_DIM, (k + 1) * HEAD_DIM)

    small = [
        pltpu.make_async_copy(ratio_in, ratio, small_sem.at[0]),
        pltpu.make_async_copy(lengths_in, lengths, small_sem.at[1]),
        pltpu.make_async_copy(partner_in, partner, small_sem.at[2]),
    ]
    at_q = half
    at_rk = at_q + lanes
    at_g = at_rk + rows
    at_pv = at_g + lanes
    at_rv = at_pv + half
    groups = ((0, at_q), (at_q, at_g), (at_g, at_rv + rows))
    small[0].start()
    small[1].start()
    for i in range(kv_local):
        loads = [(pk_in.at[:, cols_of(i)], 0, half, 0)]
        for g in range(group):
            loads.append((q_in.at[0, 0, :, cols_of(i * group + g)], at_q + g * rows, rows, 1))
        loads.append((rk_in.at[0, 0, :, cols_of(i)], at_rk, rows, 1))
        loads.append((pv_in.at[:, cols_of(i)], at_pv, half, 2))
        for g in range(group):
            loads.append((dir_in.at[0, 0, :, cols_of(i * group + g)], at_g + g * rows, rows, 2))
        loads.append((rv_in.at[0, 0, :, cols_of(i)], at_rv, rows, 2))
        for src, at, size, which in loads:
            pltpu.make_async_copy(src, held.at[i, at:at + size, :], load_sem.at[3 * i + which]).start()
    small[2].start()

    def loaded(i, which):
        with ns("loads"):
            whole = held.at[i, groups[which][0]:groups[which][1], :]
            pltpu.make_async_copy(whole, whole, load_sem.at[3 * i + which]).wait()

    def queries(i):
        return held[i, at_q:at_q + lanes, :]

    def grads(i):
        return held[i, at_g:at_g + lanes, :]

    def near_rows(i, at, name):
        at, size = (at[1], rows) if name == "resp" else (at[0] + name * part, part)
        return held[i, at:at + size, :]

    direct, relayed = {}, {}
    for i in range(kv_local):
        for which, (at, dst) in enumerate(((0, pk_far), (at_pv, pv_far))):
            slot = 2 * i + which
            shared = paired and slot > 0
            size, first = (chunk, parity * part) if shared else (part, 0)
            direct[slot], relayed[slot] = [], []
            for c in range(2):
                row = pl.multiple_of(first + c * size, size)
                span = pl.ds(row, size)
                direct[slot].append(pltpu.make_async_remote_copy(
                    src_ref=held.at[i, pl.ds(pl.multiple_of(at + row, chunk), size), :], dst_ref=dst.at[i, span, :],
                    send_sem=near_send_sem.at[slot], recv_sem=near_recv_sem.at[2 * slot + c],
                    device_id=pair_dev, device_id_type=MESH))
                if shared:
                    relayed[slot].append(pltpu.make_async_remote_copy(
                        src_ref=dst.at[i, span, :], dst_ref=dst.at[i, span, :],
                        send_sem=relay_send_sem.at[slot], recv_sem=relay_recv_sem.at[slot],
                        device_id=(side, lax.rem(seq + 1 - 2 * parity + n, n), head),
                        device_id_type=MESH))

    def whole_of(slot, send_sem, recv_sem, first):
        i, which = slot // 2, slot % 2
        span = pl.ds(pl.multiple_of(first * part, part), part)
        ref = (pk_far, pv_far)[which].at[i, span, :]
        return pltpu.make_async_remote_copy(
            src_ref=ref, dst_ref=ref, send_sem=send_sem.at[slot], recv_sem=recv_sem.at[slot],
            device_id=pair_dev, device_id_type=MESH)

    def give(slot):
        for copy in direct[slot]:
            copy.start()

    def relay(slot, c):
        with ns("relay"):
            direct[slot][c].wait_recv()
            if relayed[slot]:
                relayed[slot][c].start()

    def relay_all(slot):
        for c in range(len(direct[slot])):
            relay(slot, c)

    def wait_far(slot):
        if relayed[slot]:
            with ns("wait2"):
                whole_of(slot, relay_send_sem, relay_recv_sem, 1 - parity).wait_recv()

    def sent_far(slot):
        if relayed[slot]:
            whole_of(slot, near_send_sem, relay_recv_sem, parity).wait_send()
            whole_of(slot, relay_send_sem, relay_recv_sem, parity).wait_send()
        else:
            i, ref = slot // 2, (pk_far, pv_far)[slot % 2]
            pltpu.make_async_remote_copy(
                src_ref=ref.at[i], dst_ref=ref.at[i], send_sem=near_send_sem.at[slot],
                recv_sem=relay_recv_sem.at[slot], device_id=pair_dev, device_id_type=MESH).wait_send()

    tab_pair = pltpu.make_async_remote_copy(
        src_ref=table.at[seq, side], dst_ref=table.at[seq, side],
        send_sem=pair_sem.at[0], recv_sem=pair_sem.at[1],
        device_id=pair_dev, device_id_type=MESH)

    def tab_copy(k, way):
        turn = (1 - way) // 2
        return pltpu.make_async_remote_copy(
            src_ref=table.at[seq - way * k], dst_ref=table.at[seq - way * k],
            send_sem=tab_send_sem.at[turn], recv_sem=tab_recv_sem.at[2 * k + turn],
            device_id=seq_dev(way), device_id_type=MESH)

    def came_from(k, way):
        return (seq - way * k >= 0) & (seq - way * k < n)

    def tab_step(k):
        if k == 0:
            tab_pair.wait_recv()
        for way in (1, -1):
            if k > 0:
                @pl.when(came_from(k, way))
                def _():
                    tab_copy(k - 1, way).wait_recv()

                @pl.when(came_from(k - 1, way) & exists(way))
                def _():
                    tab_copy(k - 1, way).wait_send()
            if k < n - 1:
                @pl.when(came_from(k, way) & exists(way))
                def _():
                    tab_copy(k, way).start()

    steps = list(range(n))
    per_call = -(-(n - 1) // 3)

    def tab_some(all_left=False):
        with ns("tab"):
            for _ in range(n if all_left else per_call if steps and steps[0] else 1):
                if steps:
                    tab_step(steps.pop(0))

    def weights():
        zero = jnp.zeros((1, HEAD_DIM), F32)
        mine = partner[seq]
        rejected, chosen = zero, zero
        for r in range(n):
            rejected = rejected + jnp.where(mine == r, table[r, 1], 0.0)
            chosen = chosen + jnp.where(partner[r] == seq, table[r, 0], 0.0)
        pulled_c = 1.0 / (1.0 + jnp.exp(DPO_BETA * (table[seq, 0] - rejected)))
        pulled_r = 1.0 / (1.0 + jnp.exp(DPO_BETA * (chosen - table[seq, 1])))
        own = jnp.where(side == 0, -pulled_c, pulled_r)
        other = jnp.where(side == 0, pulled_r, -pulled_c)
        return own, other

    far_at, own_at, resp_at = 0, half, 2 * half

    def score(i, at, keys, masked=False):
        scores = dot_nt(keys, queries(i))
        if masked:
            key_pos = lax.broadcasted_iota(jnp.int32, scores.shape, 0)
            row_pos = lax.rem(lax.broadcasted_iota(jnp.int32, scores.shape, 1), rows)
            scores = jnp.where((key_pos <= row_pos) & (key_pos < length), scores, -jnp.inf)
        size = scores.shape[0]
        s_buf[i, at:at + size, :] = scores
        top = jnp.max(scores, axis=0, keepdims=True)
        shift = top * exp_scale
        total = jnp.zeros((SLAB, lanes), F32)
        for r in range(0, size, SLAB):
            span = slice(at + r, at + r + SLAB)
            e = jnp.exp2(s_buf[i, span, :] * exp_scale - shift)
            s_buf[i, span, :] = e
            total = total + e
        return top, jnp.sum(total, axis=0, keepdims=True)

    def prob_grad(i, at, values):
        dp = dot_nt(values, grads(i))
        size = dp.shape[0]
        dp_buf[i, at:at + size, :] = dp
        total = jnp.zeros((SLAB, lanes), F32)
        for r in range(0, size, SLAB):
            span = slice(at + r, at + r + SLAB)
            total = total + s_buf[i, span, :] * dp[r:r + SLAB]
        return jnp.sum(total, axis=0, keepdims=True)

    def value_grad(i, at, size, share):
        prob = (s_buf[i, at:at + size, :] * share).astype(BF16)
        return jnp.dot(prob, grads(i), preferred_element_type=F32)

    def key_grad(i, at, size, share, delta):
        ds = (s_buf[i, at:at + size, :] * share * (dp_buf[i, at:at + size, :] - delta)).astype(BF16)
        ds_buf[i, at:at + size, :] = ds
        return jnp.dot(ds, queries(i), preferred_element_type=F32)

    def unit_of(i, kind, r):
        return (2 * i + kind) * units + r

    def x_copy(u):
        return pltpu.make_async_remote_copy(
            src_ref=x_send.at[u], dst_ref=x_recv.at[u],
            send_sem=x_send_sem.at[0], recv_sem=x_recv_sem.at[u],
            device_id=pair_dev, device_id_type=MESH)

    def send_far(i, kind, b, grads):
        for k in range(per_part):
            u = unit_of(i, kind, b * per_part + k)
            x_send[u] = grads[k * unit:(k + 1) * unit].astype(BF16)
            x_copy(u).start()

    def keep_own(i, kind, b, grads):
        for k in range(per_part):
            acc[unit_of(i, kind, b * per_part + k)] = grads[k * unit:(k + 1) * unit]

    first_way = jnp.where(2 * seq < n, 1, -1)

    def chain_copy(u, way):
        turn = (1 - way) // 2
        return pltpu.make_async_remote_copy(
            src_ref=c_send.at[turn, u], dst_ref=c_recv.at[turn, u],
            send_sem=c_send_sem.at[turn], recv_sem=c_recv_sem.at[2 * u + turn],
            device_id=seq_dev(way), device_id_type=MESH)

    def chain_pass(u, way):
        turn = (1 - way) // 2
        chain_copy(u, way).wait_recv()
        c_send[turn, u] = (acc[u] + c_recv[turn, u].astype(F32)).astype(BF16)
        chain_copy(u, way).start()

    def chain_enter(u, own, other):
        factor = scale if (u // units) % 2 else 1.0
        with ns("xwait"):
            x_copy(u).wait_recv()
        acc[u] = acc[u] * (own * factor) + x_recv[u].astype(F32) * (other * factor)

        @pl.when(exists(first_way) & jnp.logical_not(exists(-first_way)))
        def _():
            c_send[(1 - first_way) // 2, u] = acc[u].astype(BF16)
            chain_copy(u, first_way).start()

    def chain_inward(u):
        @pl.when(exists(first_way) & exists(-first_way))
        def _():
            with ns("inward"):
                chain_pass(u, first_way)

    def chain_outward(u):
        @pl.when(exists(first_way) & exists(-first_way))
        def _():
            with ns("outward"):
                chain_pass(u, -first_way)
            write(u)

    def chain_end(u):
        @pl.when(jnp.logical_not(exists(-first_way)))
        def _():
            @pl.when(exists(first_way))
            def _():
                with ns("endwait"):
                    chain_copy(u, -first_way).wait_recv()
            write(u)

    def write(u):
        for way in (1, -1):
            @pl.when(exists(-way))
            def _():
                acc[u] += c_recv[(1 - way) // 2, u].astype(F32)
        i, kind, r = u // (2 * units), u // units % 2, u % units
        out = pkg_out if kind else pvg_out
        out[r * unit:(r + 1) * unit, cols_of(i)] = acc[u].astype(BF16)

    def query(i, own):
        total = jnp.zeros((HEAD_DIM, lanes), F32)
        for at, keys in (
            (own_at, held[i, :half, :]), (resp_at, held[i, at_rk:at_rk + rows, :]), (far_at, pk_far[i])
        ):
            total = total + dot_tn(keys, ds_buf[i, at:at + keys.shape[0], :])
        factor = own * scale
        for g in range(group):
            qg_out[0, 0, :, cols_of(i * group + g)] = (
                total[:, g * rows:(g + 1) * rows].T * factor).astype(BF16)

    def resp(i, own):
        rvg_out[0, 0, :, cols_of(i)] = (held_values[i] * own).astype(BF16)
        rkg_out[0, 0, :, cols_of(i)] = (
            key_grad(i, resp_at, rows, share[i, "resp"], delta[i]) * (own * scale)).astype(BF16)

    tops, totals, deltas, share, delta, held_values = {}, {}, {}, {}, {}, {}

    def resp_values(i):
        with ns(f"vresp{i}"):
            held_values[i] = value_grad(i, resp_at, rows, share[i, "resp"])

    def at_of(name):
        return resp_at if name == "resp" else own_at + name * part

    def near(i, name):
        with ns(f"near{i}{name}"):
            tops[i, name], totals[i, name] = score(
                i, at_of(name), near_rows(i, (0, at_rk), name), name == "resp")

    def near_delta(i, name):
        with ns(f"dnear{i}{name}"):
            deltas[i, name] = prob_grad(i, at_of(name), near_rows(i, (at_pv, at_rv), name))

    def far(i, b):
        with ns(f"far{i}{b}"):
            at = far_at + b * part
            tops[i, f"far{b}"], totals[i, f"far{b}"] = score(i, at, pk_far[i, b * part:(b + 1) * part, :])

    def far_delta(i, b):
        with ns(f"dfar{i}{b}"):
            at = far_at + b * part
            deltas[i, f"far{b}"] = prob_grad(i, at, pv_far[i, b * part:(b + 1) * part, :])

    names = ("far0", "far1", 0, 1, "resp")

    def stats(i):
        top = functools.reduce(jnp.maximum, [tops[i, name] for name in names])
        part_of = {name: jnp.exp2((tops[i, name] - top) * exp_scale) for name in names}
        total = sum(totals[i, name] * part_of[name] for name in names)
        row = lax.rem(lax.broadcasted_iota(jnp.int32, (1, lanes), 1), rows)
        inv = jnp.where(row < length, 1.0 / total, 0.0)
        for name in names:
            share[i, name] = part_of[name] * inv

    def far_values(i, b):
        with ns(f"vfar{i}{b}"):
            send_far(i, 0, b, value_grad(i, far_at + b * part, part, share[i, f"far{b}"]))

    def far_keys(i, b):
        with ns(f"kfar{i}{b}"):
            send_far(i, 1, b, key_grad(i, far_at + b * part, part, share[i, f"far{b}"], delta[i]))

    def own_values(i, b):
        with ns(f"vown{i}{b}"):
            keep_own(i, 0, b, value_grad(i, own_at + b * part, part, share[i, b]))

    def own_keys(i, b):
        with ns(f"kown{i}{b}"):
            keep_own(i, 1, b, key_grad(i, own_at + b * part, part, share[i, b], delta[i]))

    def sum_delta(i):
        delta[i] = sum(deltas[i, name] * share[i, name] for name in names)

    with ns("small"):
        small[0].wait()
        small[1].wait()
    length = lengths[0, 0]
    position = lax.broadcasted_iota(jnp.int32, (1, rows), 1)
    own_sum = jnp.sum(jnp.where(position < length, ratio[0], 0.0), axis=1, keepdims=True)
    table[seq, side] = jnp.broadcast_to(own_sum, (1, HEAD_DIM))
    with ns("barrier"):
        pl.semaphore_wait(barrier, 1 + jnp.where(exists(1), 1, 0) + jnp.where(exists(-1), 1, 0))
    tab_pair.start()
    loaded(0, 0)
    direct[0][0].start()
    last = kv_local - 1
    loaded(0, 1)
    near(0, 0)
    near(0, 1)
    direct[0][1].start()
    near(0, "resp")
    loaded(0, 2)
    if last:
        for which in range(3):
            loaded(last, which)
        near(last, 0)
        near(last, 1)
    give(1)
    if last:
        near(last, "resp")
    tab_some()
    near_delta(0, 0)
    near_delta(0, 1)
    near_delta(0, "resp")
    if last:
        give(2 * last)
    relay(0, 0)
    far(0, 0)
    relay(0, 1)
    far(0, 1)
    stats(0)
    if last:
        give(2 * last + 1)
    tab_some()
    far_values(0, 0)
    far_values(0, 1)
    relay_all(1)
    own_values(0, 0)
    own_values(0, 1)
    if last:
        near_delta(last, 0)
        near_delta(last, 1)
    tab_some()
    if last:
        relay_all(2 * last)
        near_delta(last, "resp")
    resp_values(0)
    if last:
        relay_all(2 * last + 1)

    weight = []

    def start_chain():
        tab_some(True)
        with ns("small"):
            small[2].wait()
        weight.extend(weights())

    def resp_work(i):
        with ns(f"resp{i}"):
            resp(i, weight[0])

    def query_work(i):
        with ns(f"query{i}"):
            query(i, weight[0])

    work = [
        (0.3, lambda: (wait_far(1), far_delta(0, 0))), (0.3, lambda: (far_delta(0, 1), sum_delta(0))),
        (0.3, lambda: far_keys(0, 0)), (0.3, lambda: far_keys(0, 1)),
    ]
    work += [(0.3, lambda: own_keys(0, 0)), (0.3, lambda: own_keys(0, 1))]
    if last:
        work += [
            (0.5, lambda: (wait_far(2 * last), far(last, 0))), (0.5, lambda: (far(last, 1), stats(last))),
            (0.3, lambda: far_values(last, 0)), (0.3, lambda: far_values(last, 1)),
            (0.3, lambda: (wait_far(2 * last + 1), far_delta(last, 0))),
            (0.3, lambda: (far_delta(last, 1), sum_delta(last))),
            (0.3, lambda: far_keys(last, 0)), (0.3, lambda: far_keys(last, 1)),
            (0.3, lambda: own_values(last, 0)), (0.3, lambda: own_values(last, 1)),
            (0.3, lambda: own_keys(last, 0)), (0.3, lambda: own_keys(last, 1)),
        ]
    if last:
        work += [(0.2, lambda: resp_values(last))]
    work += [(0.3, lambda i=i: resp_work(i)) for i in range(kv_local)]
    work += [(0.65, lambda i=i: query_work(i)) for i in range(kv_local)]
    chain = []
    for u in range(count):
        for hops, step in enumerate((chain_enter, chain_inward, chain_outward, chain_end)):
            chain.append((LEAD + u * RATE + hops * HOP, hops, u, step))
    chain.sort(key=lambda item: item[:3])
    now = 0.0
    while work or chain:
        if chain and (not work or chain[0][0] <= now):
            at, hops, u, step = chain.pop(0)
            now = max(now, at) + 0.04
            if not weight:
                start_chain()
            if hops == 0:
                step(u, *weight)
            else:
                step(u)
        else:
            cost, step = work.pop(0)
            step()
            now += cost

    with ns("sendwait"):
        tab_pair.wait_send()
        for slot_ in range(2 * kv_local):
            sent_far(slot_)
        pltpu.make_async_remote_copy(
            src_ref=x_send, dst_ref=x_recv, send_sem=x_send_sem.at[0], recv_sem=x_recv_sem.at[0],
            device_id=pair_dev, device_id_type=MESH).wait_send()
        for way in (1, -1):
            @pl.when(exists(way))
            def _():
                turn = (1 - way) // 2
                pltpu.make_async_remote_copy(
                    src_ref=c_send.at[turn], dst_ref=c_recv.at[turn],
                    send_sem=c_send_sem.at[turn], recv_sem=c_recv_sem.at[0],
                    device_id=seq_dev(way), device_id_type=MESH).wait_send()


def store_kernel(count, *refs):
    sources, targets, sem = refs[:count], refs[count:2 * count], refs[2 * count]
    stores = [pltpu.make_async_copy(sources[k], targets[k], sem.at[k]) for k in range(count)]
    for store in stores:
        store.start()
    for store in stores:
        store.wait()


def store_all(arrays):
    count = len(arrays)
    return pl.pallas_call(
        functools.partial(store_kernel, count),
        out_shape=tuple(jax.ShapeDtypeStruct(a.shape, a.dtype) for a in arrays),
        in_specs=[pl.BlockSpec(memory_space=pltpu.VMEM)] * count,
        out_specs=(pl.BlockSpec(memory_space=pl.ANY),) * count,
        scratch_shapes=[pltpu.SemaphoreType.DMA((count,))],
        compiler_params=pltpu.CompilerParams(vmem_limit_bytes=1024 * 1024),
        name="store_results",
    )(*arrays)


def shards(
    n, resp_query, resp_key, resp_value, direction, ratio, lengths, partner, prompt_key, prompt_value
):
    rows = resp_query.shape[2]
    half, key_width = prompt_key.shape
    kv_local = key_width // HEAD_DIM
    heads = resp_query.shape[3] // HEAD_DIM
    lanes = rows * heads // kv_local
    keys = 2 * half + rows
    unit = sizes(n, half)[-1]
    count = 2 * kv_local * (half // unit)
    hbm = pl.BlockSpec(memory_space=pltpu.HBM)
    dma = pltpu.SemaphoreType.DMA
    results = pl.pallas_call(
        functools.partial(kernel, n),
        out_shape=tuple(
            pltpu.VMEM(a.shape, BF16)
            for a in (resp_query, resp_key, resp_value, prompt_key, prompt_value)
        ),
        in_specs=[hbm] * 9,
        scratch_shapes=[
            pltpu.SMEM((1, 1), jnp.int32),
            pltpu.SMEM((n,), jnp.int32),
            pltpu.VMEM((1, 1, rows), F32),
            pltpu.VMEM((n, 2, 1, HEAD_DIM), F32),
            pltpu.VMEM((kv_local, 2 * (half + lanes + rows), HEAD_DIM), BF16),
            pltpu.VMEM((kv_local, half, HEAD_DIM), BF16),
            pltpu.VMEM((kv_local, half, HEAD_DIM), BF16),
            pltpu.VMEM((kv_local, keys, lanes), F32),
            pltpu.VMEM((kv_local, keys, lanes), F32),
            pltpu.VMEM((kv_local, keys, lanes), BF16),
            pltpu.VMEM((count, unit, HEAD_DIM), BF16),
            pltpu.VMEM((count, unit, HEAD_DIM), BF16),
            pltpu.VMEM((count, unit, HEAD_DIM), F32),
            pltpu.VMEM((2, count, unit, HEAD_DIM), BF16),
            pltpu.VMEM((2, count, unit, HEAD_DIM), BF16),
            dma((3,)), dma((3 * kv_local,)), dma((2,)), dma((2 * max(n - 1, 1),)), dma((2,)),
            dma((2 * kv_local,)), dma((4 * kv_local,)), dma((2 * kv_local,)), dma((2 * kv_local,)),
            dma((1,)), dma((count,)), dma((2,)), dma((2 * count,)),
        ],
        compiler_params=pltpu.CompilerParams(
            collective_id=0, has_side_effects=True, vmem_limit_bytes=48 * 1024 * 1024
        ),
        name="shared_prompt_backward",
    )(lengths, *(
        pltpu.with_memory_space_constraint(a, pltpu.HBM)
        for a in (partner, ratio, resp_query, resp_key, resp_value, direction, prompt_key, prompt_value)
    ))
    return store_all(results)


def solution(mesh):
    per_response = P("pair", "seq", None, "head")
    per_prompt = P("pair", "head")
    in_specs = (
        per_response, per_response, per_response, per_response,
        P("pair", "seq", None), P("pair", "seq"), P(), per_prompt, per_prompt,
    )
    out_specs = (per_response, per_response, per_response, per_prompt, per_prompt)
    return jax.shard_map(
        functools.partial(shards, mesh.shape["seq"]),
        mesh=mesh, in_specs=in_specs, out_specs=out_specs, check_vma=False,
    )
```

```python
import functools
import math

import jax
import jax.numpy as jnp
from jax import lax
from jax.experimental import pallas as pl
from jax.experimental.pallas import tpu as pltpu
from jax.sharding import PartitionSpec as P

HEAD_DIM = 128
DPO_BETA = 0.1
UNIT = 128
SLAB = 8
RATE, HOP, LEAD = 0.7, 3.5, 0.6
MESH = pl.DeviceIdType.MESH
NT = (((1,), (1,)), ((), ()))
TN = (((0,), (0,)), ((), ()))
F32 = jnp.float32
BF16 = jnp.bfloat16


def dot_nt(a, b):
    return lax.dot_general(a, b, NT, preferred_element_type=F32)


def dot_tn(a, b):
    return lax.dot_general(a, b, TN, preferred_element_type=F32)


def sizes(n, half):
    paired = n % 2 == 0
    part = half // 2
    return paired, part, part // 2, min(UNIT, part)


def kernel(
    n, lengths_in, partner_in, ratio_in, q_in, rk_in, rv_in, dir_in, pk_in, pv_in,
    qg_out, rkg_out, rvg_out, pkg_out, pvg_out,
    partner, ratio, table, held, pk_far, pv_far,
    s_buf, dp_buf, ds_buf, x_send, x_recv, acc, c_send, c_recv,
    small_sem, load_sem, tab_send_sem, tab_recv_sem, pair_sem,
    near_send_sem, near_recv_sem, relay_send_sem, relay_recv_sem,
    x_send_sem, x_recv_sem, c_send_sem, c_recv_sem,
):
    ns = jax.named_scope
    rows = q_in.shape[2]
    half = pk_in.shape[0]
    kv_local = rk_in.shape[3] // HEAD_DIM
    group = q_in.shape[3] // rk_in.shape[3]
    lanes = rows * group
    paired, part, chunk, unit = sizes(n, half)
    units = half // unit
    per_part = part // unit
    count = 2 * kv_local * units
    scale = 1.0 / math.sqrt(HEAD_DIM)
    exp_scale = scale * math.log2(math.e)
    side = lax.axis_index("pair")
    seq = lax.axis_index("seq")
    head = lax.axis_index("head")
    flat = side * n + seq
    parity = lax.rem(seq, 2)
    pair_dev = (1 - side, seq, head)

    def seq_dev(way):
        return (side, lax.rem(seq + way + n, n), head)

    def exists(way):
        return (seq + way >= 0) & (seq + way < n)

    barrier = pltpu.get_barrier_semaphore()
    pl.semaphore_signal(barrier, inc=1, device_id=pair_dev, device_id_type=MESH)
    for way in (1, -1):
        @pl.when(exists(way))
        def _():
            pl.semaphore_signal(barrier, inc=1, device_id=seq_dev(way), device_id_type=MESH)

    def cols_of(k):
        return slice(k * HEAD_DIM, (k + 1) * HEAD_DIM)

    small = [
        pltpu.make_async_copy(ratio_in, ratio, small_sem.at[0]),
        pltpu.make_async_copy(partner_in, partner, small_sem.at[1]),
    ]
    at_q = half
    at_rk = at_q + lanes
    at_g = at_rk + rows
    at_pv = at_g + lanes
    at_rv = at_pv + half
    groups = ((0, at_q), (at_q, at_g), (at_g, at_rv + rows))
    small[0].start()
    for i in range(kv_local):
        loads = [(pk_in.at[:, cols_of(i)], 0, half, 0)]
        for g in range(group):
            loads.append((q_in.at[0, 0, :, cols_of(i * group + g)], at_q + g * rows, rows, 1))
        loads.append((rk_in.at[0, 0, :, cols_of(i)], at_rk, rows, 1))
        loads.append((pv_in.at[:, cols_of(i)], at_pv, half, 2))
        for g in range(group):
            loads.append((dir_in.at[0, 0, :, cols_of(i * group + g)], at_g + g * rows, rows, 2))
        loads.append((rv_in.at[0, 0, :, cols_of(i)], at_rv, rows, 2))
        for src, at, size, which in loads:
            pltpu.make_async_copy(src, held.at[i, at:at + size, :], load_sem.at[3 * i + which]).start()
    small[1].start()

    def loaded(i, which):
        with ns("loads"):
            whole = held.at[i, groups[which][0]:groups[which][1], :]
            pltpu.make_async_copy(whole, whole, load_sem.at[3 * i + which]).wait()

    def queries(i):
        return held[i, at_q:at_q + lanes, :]

    def grads(i):
        return held[i, at_g:at_g + lanes, :]

    def near_rows(i, at, name):
        at, size = (at[1], rows) if name == "resp" else (at[0] + name * part, part)
        return held[i, at:at + size, :]

    direct, relayed = {}, {}
    for i in range(kv_local):
        for which, (at, dst) in enumerate(((0, pk_far), (at_pv, pv_far))):
            slot = 2 * i + which
            shared = paired and slot > 0
            size, first = (chunk, parity * part) if shared else (part, 0)
            direct[slot], relayed[slot] = [], []
            for c in range(2):
                row = pl.multiple_of(first + c * size, size)
                span = pl.ds(row, size)
                direct[slot].append(pltpu.make_async_remote_copy(
                    src_ref=held.at[i, pl.ds(pl.multiple_of(at + row, chunk), size), :], dst_ref=dst.at[i, span, :],
                    send_sem=near_send_sem.at[slot], recv_sem=near_recv_sem.at[2 * slot + c],
                    device_id=pair_dev, device_id_type=MESH))
                if shared:
                    relayed[slot].append(pltpu.make_async_remote_copy(
                        src_ref=dst.at[i, span, :], dst_ref=dst.at[i, span, :],
                        send_sem=relay_send_sem.at[slot], recv_sem=relay_recv_sem.at[slot],
                        device_id=(side, lax.rem(seq + 1 - 2 * parity + n, n), head),
                        device_id_type=MESH))

    def whole_of(slot, send_sem, recv_sem, first):
        i, which = slot // 2, slot % 2
        span = pl.ds(pl.multiple_of(first * part, part), part)
        ref = (pk_far, pv_far)[which].at[i, span, :]
        return pltpu.make_async_remote_copy(
            src_ref=ref, dst_ref=ref, send_sem=send_sem.at[slot], recv_sem=recv_sem.at[slot],
            device_id=pair_dev, device_id_type=MESH)

    def give(slot):
        for copy in direct[slot]:
            copy.start()

    def relay(slot, c):
        with ns("relay"):
            direct[slot][c].wait_recv()
            if relayed[slot]:
                relayed[slot][c].start()

    def relay_all(slot):
        for c in range(len(direct[slot])):
            relay(slot, c)

    def wait_far(slot):
        if relayed[slot]:
            with ns("wait2"):
                whole_of(slot, relay_send_sem, relay_recv_sem, 1 - parity).wait_recv()

    def sent_far(slot):
        if relayed[slot]:
            whole_of(slot, near_send_sem, relay_recv_sem, parity).wait_send()
            whole_of(slot, relay_send_sem, relay_recv_sem, parity).wait_send()
        else:
            i, ref = slot // 2, (pk_far, pv_far)[slot % 2]
            pltpu.make_async_remote_copy(
                src_ref=ref.at[i], dst_ref=ref.at[i], send_sem=near_send_sem.at[slot],
                recv_sem=relay_recv_sem.at[slot], device_id=pair_dev, device_id_type=MESH).wait_send()

    tab_pair = pltpu.make_async_remote_copy(
        src_ref=table.at[seq, side], dst_ref=table.at[seq, side],
        send_sem=pair_sem.at[0], recv_sem=pair_sem.at[1],
        device_id=pair_dev, device_id_type=MESH)

    def tab_copy(k, way):
        turn = (1 - way) // 2
        return pltpu.make_async_remote_copy(
            src_ref=table.at[seq - way * k], dst_ref=table.at[seq - way * k],
            send_sem=tab_send_sem.at[turn], recv_sem=tab_recv_sem.at[2 * k + turn],
            device_id=seq_dev(way), device_id_type=MESH)

    def came_from(k, way):
        return (seq - way * k >= 0) & (seq - way * k < n)

    def tab_step(k):
        if k == 0:
            tab_pair.wait_recv()
        for way in (1, -1):
            if k > 0:
                @pl.when(came_from(k, way))
                def _():
                    tab_copy(k - 1, way).wait_recv()

                @pl.when(came_from(k - 1, way) & exists(way))
                def _():
                    tab_copy(k - 1, way).wait_send()
            if k < n - 1:
                @pl.when(came_from(k, way) & exists(way))
                def _():
                    tab_copy(k, way).start()

    steps = list(range(n))
    per_call = -(-(n - 1) // 3)

    def tab_some(all_left=False):
        with ns("tab"):
            for _ in range(n if all_left else per_call if steps and steps[0] else 1):
                if steps:
                    tab_step(steps.pop(0))

    def weights():
        zero = jnp.zeros((1, HEAD_DIM), F32)
        mine = partner[seq]
        rejected, chosen = zero, zero
        for r in range(n):
            rejected = rejected + jnp.where(mine == r, table[r, 1], 0.0)
            chosen = chosen + jnp.where(partner[r] == seq, table[r, 0], 0.0)
        pulled_c = 1.0 / (1.0 + jnp.exp(DPO_BETA * (table[seq, 0] - rejected)))
        pulled_r = 1.0 / (1.0 + jnp.exp(DPO_BETA * (chosen - table[seq, 1])))
        own = jnp.where(side == 0, -pulled_c, pulled_r)
        other = jnp.where(side == 0, pulled_r, -pulled_c)
        return own, other

    far_at, own_at, resp_at = 0, half, 2 * half

    def score(i, at, keys, masked=False):
        scores = dot_nt(keys, queries(i))
        if masked:
            key_pos = lax.broadcasted_iota(jnp.int32, scores.shape, 0)
            row_pos = lax.rem(lax.broadcasted_iota(jnp.int32, scores.shape, 1), rows)
            scores = jnp.where((key_pos <= row_pos) & (key_pos < length), scores, -jnp.inf)
        size = scores.shape[0]
        s_buf[i, at:at + size, :] = scores
        top = jnp.max(scores, axis=0, keepdims=True)
        shift = top * exp_scale
        total = jnp.zeros((SLAB, lanes), F32)
        for r in range(0, size, SLAB):
            span = slice(at + r, at + r + SLAB)
            e = jnp.exp2(s_buf[i, span, :] * exp_scale - shift)
            s_buf[i, span, :] = e
            total = total + e
        return top, jnp.sum(total, axis=0, keepdims=True)

    def prob_grad(i, at, values):
        dp = dot_nt(values, grads(i))
        size = dp.shape[0]
        dp_buf[i, at:at + size, :] = dp
        total = jnp.zeros((SLAB, lanes), F32)
        for r in range(0, size, SLAB):
            span = slice(at + r, at + r + SLAB)
            total = total + s_buf[i, span, :] * dp[r:r + SLAB]
        return jnp.sum(total, axis=0, keepdims=True)

    def value_grad(i, at, size, share):
        prob = (s_buf[i, at:at + size, :] * share).astype(BF16)
        return jnp.dot(prob, grads(i), preferred_element_type=F32)

    def key_grad(i, at, size, share, delta):
        ds = (s_buf[i, at:at + size, :] * share * (dp_buf[i, at:at + size, :] - delta)).astype(BF16)
        ds_buf[i, at:at + size, :] = ds
        return jnp.dot(ds, queries(i), preferred_element_type=F32)

    def unit_of(i, kind, r):
        return (2 * i + kind) * units + r

    def x_copy(u):
        return pltpu.make_async_remote_copy(
            src_ref=x_send.at[u], dst_ref=x_recv.at[u],
            send_sem=x_send_sem.at[0], recv_sem=x_recv_sem.at[u],
            device_id=pair_dev, device_id_type=MESH)

    def send_far(i, kind, b, grads):
        for k in range(per_part):
            u = unit_of(i, kind, b * per_part + k)
            x_send[u] = grads[k * unit:(k + 1) * unit].astype(BF16)
            x_copy(u).start()

    def keep_own(i, kind, b, grads):
        for k in range(per_part):
            acc[unit_of(i, kind, b * per_part + k)] = grads[k * unit:(k + 1) * unit]

    first_way = jnp.where(2 * seq < n, 1, -1)

    def chain_copy(u, way):
        turn = (1 - way) // 2
        return pltpu.make_async_remote_copy(
            src_ref=c_send.at[turn, u], dst_ref=c_recv.at[turn, u],
            send_sem=c_send_sem.at[turn], recv_sem=c_recv_sem.at[2 * u + turn],
            device_id=seq_dev(way), device_id_type=MESH)

    def chain_pass(u, way):
        turn = (1 - way) // 2
        chain_copy(u, way).wait_recv()
        c_send[turn, u] = (acc[u] + c_recv[turn, u].astype(F32)).astype(BF16)
        chain_copy(u, way).start()

    def chain_enter(u, own, other):
        factor = scale if (u // units) % 2 else 1.0
        with ns("xwait"):
            x_copy(u).wait_recv()
        acc[u] = acc[u] * (own * factor) + x_recv[u].astype(F32) * (other * factor)

        @pl.when(exists(first_way) & jnp.logical_not(exists(-first_way)))
        def _():
            c_send[(1 - first_way) // 2, u] = acc[u].astype(BF16)
            chain_copy(u, first_way).start()

    def chain_inward(u):
        @pl.when(exists(first_way) & exists(-first_way))
        def _():
            with ns("inward"):
                chain_pass(u, first_way)

    def chain_outward(u):
        @pl.when(exists(first_way) & exists(-first_way))
        def _():
            with ns("outward"):
                chain_pass(u, -first_way)
            write(u)

    def chain_end(u):
        @pl.when(jnp.logical_not(exists(-first_way)))
        def _():
            @pl.when(exists(first_way))
            def _():
                with ns("endwait"):
                    chain_copy(u, -first_way).wait_recv()
            write(u)

    def write(u):
        for way in (1, -1):
            @pl.when(exists(-way))
            def _():
                acc[u] += c_recv[(1 - way) // 2, u].astype(F32)
        i, kind, r = u // (2 * units), u // units % 2, u % units
        out = pkg_out if kind else pvg_out
        out[r * unit:(r + 1) * unit, cols_of(i)] = acc[u].astype(BF16)

    def query(i, own):
        total = jnp.zeros((HEAD_DIM, lanes), F32)
        for at, keys in (
            (own_at, held[i, :half, :]), (resp_at, held[i, at_rk:at_rk + rows, :]), (far_at, pk_far[i])
        ):
            total = total + dot_tn(keys, ds_buf[i, at:at + keys.shape[0], :])
        factor = own * scale
        for g in range(group):
            qg_out[0, 0, :, cols_of(i * group + g)] = (
                total[:, g * rows:(g + 1) * rows].T * factor).astype(BF16)

    def resp(i, own):
        rvg_out[0, 0, :, cols_of(i)] = (held_values[i] * own).astype(BF16)
        rkg_out[0, 0, :, cols_of(i)] = (
            key_grad(i, resp_at, rows, share[i, "resp"], delta[i]) * (own * scale)).astype(BF16)

    tops, totals, deltas, share, delta, held_values = {}, {}, {}, {}, {}, {}

    def resp_values(i):
        with ns(f"vresp{i}"):
            held_values[i] = value_grad(i, resp_at, rows, share[i, "resp"])

    def at_of(name):
        return resp_at if name == "resp" else own_at + name * part

    def near(i, name):
        with ns(f"near{i}{name}"):
            tops[i, name], totals[i, name] = score(
                i, at_of(name), near_rows(i, (0, at_rk), name), name == "resp")

    def near_delta(i, name):
        with ns(f"dnear{i}{name}"):
            deltas[i, name] = prob_grad(i, at_of(name), near_rows(i, (at_pv, at_rv), name))

    def far(i, b):
        with ns(f"far{i}{b}"):
            at = far_at + b * part
            tops[i, f"far{b}"], totals[i, f"far{b}"] = score(i, at, pk_far[i, b * part:(b + 1) * part, :])

    def far_delta(i, b):
        with ns(f"dfar{i}{b}"):
            at = far_at + b * part
            deltas[i, f"far{b}"] = prob_grad(i, at, pv_far[i, b * part:(b + 1) * part, :])

    names = ("far0", "far1", 0, 1, "resp")

    def stats(i):
        top = functools.reduce(jnp.maximum, [tops[i, name] for name in names])
        part_of = {name: jnp.exp2((tops[i, name] - top) * exp_scale) for name in names}
        total = sum(totals[i, name] * part_of[name] for name in names)
        row = lax.rem(lax.broadcasted_iota(jnp.int32, (1, lanes), 1), rows)
        inv = jnp.where(row < length, 1.0 / total, 0.0)
        for name in names:
            share[i, name] = part_of[name] * inv

    def far_values(i, b):
        with ns(f"vfar{i}{b}"):
            send_far(i, 0, b, value_grad(i, far_at + b * part, part, share[i, f"far{b}"]))

    def far_keys(i, b):
        with ns(f"kfar{i}{b}"):
            send_far(i, 1, b, key_grad(i, far_at + b * part, part, share[i, f"far{b}"], delta[i]))

    def own_values(i, b):
        with ns(f"vown{i}{b}"):
            keep_own(i, 0, b, value_grad(i, own_at + b * part, part, share[i, b]))

    def own_keys(i, b):
        with ns(f"kown{i}{b}"):
            keep_own(i, 1, b, key_grad(i, own_at + b * part, part, share[i, b], delta[i]))

    def sum_delta(i):
        delta[i] = sum(deltas[i, name] * share[i, name] for name in names)

    with ns("small"):
        small[0].wait()
    length = lengths_in[0, 0]
    position = lax.broadcasted_iota(jnp.int32, (1, rows), 1)
    own_sum = jnp.sum(jnp.where(position < length, ratio[0], 0.0), axis=1, keepdims=True)
    table[seq, side] = jnp.broadcast_to(own_sum, (1, HEAD_DIM))
    with ns("barrier"):
        pl.semaphore_wait(barrier, 1 + jnp.where(exists(1), 1, 0) + jnp.where(exists(-1), 1, 0))
    tab_pair.start()
    loaded(0, 0)
    direct[0][0].start()
    last = kv_local - 1
    loaded(0, 1)
    near(0, 0)
    near(0, 1)
    direct[0][1].start()
    near(0, "resp")
    loaded(0, 2)
    give(1)
    if last:
        for which in range(3):
            loaded(last, which)
        near(last, 0)
        near(last, 1)
    if last:
        near(last, "resp")
    tab_some()
    near_delta(0, 0)
    near_delta(0, 1)
    near_delta(0, "resp")
    if last:
        give(2 * last)
    relay(0, 0)
    far(0, 0)
    relay(0, 1)
    far(0, 1)
    stats(0)
    if last:
        give(2 * last + 1)
    tab_some()
    far_values(0, 0)
    far_values(0, 1)
    relay_all(1)
    own_values(0, 0)
    own_values(0, 1)
    if last:
        near_delta(last, 0)
        near_delta(last, 1)
    tab_some()
    if last:
        relay_all(2 * last)
        near_delta(last, "resp")
    resp_values(0)
    if last:
        relay_all(2 * last + 1)

    weight = []

    def start_chain():
        tab_some(True)
        with ns("small"):
            small[1].wait()
        weight.extend(weights())

    def resp_work(i):
        with ns(f"resp{i}"):
            resp(i, weight[0])

    def query_work(i):
        with ns(f"query{i}"):
            query(i, weight[0])

    work = [
        (0.3, lambda: (wait_far(1), far_delta(0, 0))), (0.3, lambda: (far_delta(0, 1), sum_delta(0))),
        (0.3, lambda: far_keys(0, 0)), (0.3, lambda: far_keys(0, 1)),
    ]
    work += [(0.3, lambda: own_keys(0, 0)), (0.3, lambda: own_keys(0, 1))]
    if last:
        work += [
            (0.5, lambda: (wait_far(2 * last), far(last, 0))), (0.5, lambda: (far(last, 1), stats(last))),
            (0.3, lambda: far_values(last, 0)), (0.3, lambda: far_values(last, 1)),
            (0.3, lambda: (wait_far(2 * last + 1), far_delta(last, 0))),
            (0.3, lambda: (far_delta(last, 1), sum_delta(last))),
            (0.3, lambda: far_keys(last, 0)), (0.3, lambda: far_keys(last, 1)),
            (0.3, lambda: own_values(last, 0)), (0.3, lambda: own_values(last, 1)),
            (0.3, lambda: own_keys(last, 0)), (0.3, lambda: own_keys(last, 1)),
        ]
    if last:
        work += [(0.2, lambda: resp_values(last))]
    work += [(0.3, lambda i=i: resp_work(i)) for i in range(kv_local)]
    work += [(0.65, lambda i=i: query_work(i)) for i in range(kv_local)]
    chain = []
    for u in range(count):
        for hops, step in enumerate((chain_enter, chain_inward, chain_outward, chain_end)):
            chain.append((LEAD + u * RATE + hops * HOP, hops, u, step))
    chain.sort(key=lambda item: item[:3])
    now = 0.0
    while work or chain:
        if chain and (not work or chain[0][0] <= now):
            at, hops, u, step = chain.pop(0)
            now = max(now, at) + 0.04
            if not weight:
                start_chain()
            if hops == 0:
                step(u, *weight)
            else:
                step(u)
        else:
            cost, step = work.pop(0)
            step()
            now += cost

    with ns("sendwait"):
        tab_pair.wait_send()
        for slot_ in range(2 * kv_local):
            sent_far(slot_)
        pltpu.make_async_remote_copy(
            src_ref=x_send, dst_ref=x_recv, send_sem=x_send_sem.at[0], recv_sem=x_recv_sem.at[0],
            device_id=pair_dev, device_id_type=MESH).wait_send()
        for way in (1, -1):
            @pl.when(exists(way))
            def _():
                turn = (1 - way) // 2
                pltpu.make_async_remote_copy(
                    src_ref=c_send.at[turn], dst_ref=c_recv.at[turn],
                    send_sem=c_send_sem.at[turn], recv_sem=c_recv_sem.at[0],
                    device_id=seq_dev(way), device_id_type=MESH).wait_send()


def store_kernel(count, *refs):
    sources, targets, sem = refs[:count], refs[count:2 * count], refs[2 * count]
    stores = [pltpu.make_async_copy(sources[k], targets[k], sem.at[k]) for k in range(count)]
    for store in stores:
        store.start()
    for store in stores:
        store.wait()


def store_all(arrays):
    count = len(arrays)
    return pl.pallas_call(
        functools.partial(store_kernel, count),
        out_shape=tuple(jax.ShapeDtypeStruct(a.shape, a.dtype) for a in arrays),
        in_specs=[pl.BlockSpec(memory_space=pltpu.VMEM)] * count,
        out_specs=(pl.BlockSpec(memory_space=pl.ANY),) * count,
        scratch_shapes=[pltpu.SemaphoreType.DMA((count,))],
        compiler_params=pltpu.CompilerParams(vmem_limit_bytes=1024 * 1024),
        name="store_results",
    )(*arrays)


def shards(
    n, resp_query, resp_key, resp_value, direction, ratio, lengths, partner, prompt_key, prompt_value
):
    rows = resp_query.shape[2]
    half, key_width = prompt_key.shape
    kv_local = key_width // HEAD_DIM
    heads = resp_query.shape[3] // HEAD_DIM
    lanes = rows * heads // kv_local
    keys = 2 * half + rows
    unit = sizes(n, half)[-1]
    count = 2 * kv_local * (half // unit)
    hbm = pl.BlockSpec(memory_space=pltpu.HBM)
    dma = pltpu.SemaphoreType.DMA
    results = pl.pallas_call(
        functools.partial(kernel, n),
        out_shape=tuple(
            pltpu.VMEM(a.shape, BF16)
            for a in (resp_query, resp_key, resp_value, prompt_key, prompt_value)
        ),
        in_specs=[pl.BlockSpec(memory_space=pltpu.SMEM)] + [hbm] * 8,
        scratch_shapes=[
            pltpu.SMEM((n,), jnp.int32),
            pltpu.VMEM((1, 1, rows), F32),
            pltpu.VMEM((n, 2, 1, HEAD_DIM), F32),
            pltpu.VMEM((kv_local, 2 * (half + lanes + rows), HEAD_DIM), BF16),
            pltpu.VMEM((kv_local, half, HEAD_DIM), BF16),
            pltpu.VMEM((kv_local, half, HEAD_DIM), BF16),
            pltpu.VMEM((kv_local, keys, lanes), F32),
            pltpu.VMEM((kv_local, keys, lanes), F32),
            pltpu.VMEM((kv_local, keys, lanes), BF16),
            pltpu.VMEM((count, unit, HEAD_DIM), BF16),
            pltpu.VMEM((count, unit, HEAD_DIM), BF16),
            pltpu.VMEM((count, unit, HEAD_DIM), F32),
            pltpu.VMEM((2, count, unit, HEAD_DIM), BF16),
            pltpu.VMEM((2, count, unit, HEAD_DIM), BF16),
            dma((2,)), dma((3 * kv_local,)), dma((2,)), dma((2 * max(n - 1, 1),)), dma((2,)),
            dma((2 * kv_local,)), dma((4 * kv_local,)), dma((2 * kv_local,)), dma((2 * kv_local,)),
            dma((1,)), dma((count,)), dma((2,)), dma((2 * count,)),
        ],
        compiler_params=pltpu.CompilerParams(
            collective_id=0, has_side_effects=True, vmem_limit_bytes=48 * 1024 * 1024
        ),
        name="shared_prompt_backward",
    )(lengths, *(
        pltpu.with_memory_space_constraint(a, pltpu.HBM)
        for a in (partner, ratio, resp_query, resp_key, resp_value, direction, prompt_key, prompt_value)
    ))
    return store_all(results)


def solution(mesh):
    per_response = P("pair", "seq", None, "head")
    per_prompt = P("pair", "head")
    in_specs = (
        per_response, per_response, per_response, per_response,
        P("pair", "seq", None), P("pair", "seq"), P(), per_prompt, per_prompt,
    )
    out_specs = (per_response, per_response, per_response, per_prompt, per_prompt)
    return jax.shard_map(
        functools.partial(shards, mesh.shape["seq"]),
        mesh=mesh, in_specs=in_specs, out_specs=out_specs, check_vma=False,
    )
```
